256 devices in a mesh: gx: 4 (over y), gy: 4 (over z_hi, core), gz: 16 (over z_lo, x).
Axes of the slice: x: 4, y: 4, z: 8 (z_hi: 2, z_lo: 4; z = z_hi * 4 + z_lo), core: 2. Of those that a mesh axis runs over, the one named last changes fastest.
Arguments:
- currents: float32 [131072, 512], P(('gx', 'gy', 'gz')), may hold values from -6 to 6
Outputs:
- power_spectra: float32 [256, 512, 512], P(('gx', 'gy', 'gz'))
- cross_spectra: float32 [256, 512, 512], P(('gx', 'gy', 'gz'))
The draws below stay inside these ranges and needn't reach their ends.
All inputs are finite; a program needn't handle non-finite values.
Results may differ from the reference program's by a relative error of at most 0.00014.
Values sent between devices are 32-bit elements; how exact they have to be, the bound alone decides.
A program may use at most 64 MiB of HBM per device.

```python
import jax
import jax.numpy as jnp
from jax import lax

MODES = 512
BIN_WIDTH = 256
STEPS = 131072
FREQS = 65536
BINS = 256


def block_levels(key, extent, shards, smallest, high):
    factor_of, own = 1.0, jax.random.fold_in(key, 6)
    for position, shards_of in shards:
        heights = jnp.exp(jax.random.uniform(jax.random.fold_in(own, position), (shards_of,), jnp.float32, smallest / len(shards), high / len(shards)))
        factor_of = factor_of * jnp.repeat(heights, extent[position] // shards_of).reshape([-1 if axis == position else 1 for axis in range(len(extent))])
    return factor_of


def normal_values(stream_key, shape, spread, most, cuts=(), kind=jnp.bfloat16):
    drawn = jax.random.normal(stream_key, shape, jnp.float32) * spread
    if len(cuts) > 0:
        drawn = block_levels(stream_key, shape, cuts, -0.22, 0.18) * drawn
    return jnp.clip(drawn, min=-most, max=most).astype(kind)


def setup_inputs(seed: int = 0) -> dict:
    streams_of = jax.random.split(jax.random.key(seed), 2)
    return {
        "currents": normal_values(streams_of[0], (STEPS, MODES), 1.0, 6.0, ((0, 256),), jnp.float32),
    }


def reference(currents):
    spectrum = jnp.fft.rfft(currents, axis=0)[:FREQS]
    real_rows = jnp.real(spectrum).reshape(BINS, BIN_WIDTH, MODES)
    imag_rows = jnp.imag(spectrum).reshape(BINS, BIN_WIDTH, MODES)
    scaling = 1.0 / (float(STEPS) * float(BIN_WIDTH))

    def one_bin(pair_rows):
        real_part, imag_part = pair_rows
        power_sum = jnp.dot(real_part.T, real_part, precision=lax.Precision.HIGHEST, preferred_element_type=jnp.float32)
        power_sum = power_sum + jnp.dot(imag_part.T, imag_part, precision=lax.Precision.HIGHEST, preferred_element_type=jnp.float32)
        cross_sum = jnp.dot(imag_part.T, real_part, precision=lax.Precision.HIGHEST, preferred_element_type=jnp.float32)
        return power_sum * scaling, (cross_sum - cross_sum.T) * scaling

    power_spectra, cross_spectra = lax.map(one_bin, (real_rows, imag_rows))
    return power_spectra, cross_spectra
```

```python
import jax
import jax.numpy as jnp
import numpy as np
from jax import lax
from jax.experimental import pallas as pl
from jax.experimental.pallas import tpu as pltpu
from jax.sharding import PartitionSpec as P

MESH = pl.DeviceIdType.MESH
AXES = ("gx", "gy", "gz")
STEPS = 131072
F32, BF16 = jnp.float32, jnp.bfloat16
Z_ORDER = [(d * s, c) for d in (1, 2, 3) for c in (0, 1) for s in (1, -1)] + [(4, 0), (4, 1), (0, 1)]
XY_ORDER = [
    (1, 0), (-1, 0), (0, 1), (0, -1), (1, 1), (-1, -1), (1, -1), (-1, 1),
    (2, 1), (1, 2), (2, -1), (-1, 2), (2, 0), (0, 2), (2, 2),
]


def halves(table):
    high = np.asarray(table, np.float32).astype(jnp.bfloat16)
    low = (np.asarray(table, np.float32) - high.astype(np.float32)).astype(jnp.bfloat16)
    return np.stack([high, low])


def tables():
    position = np.arange(256)
    xy, zc = position // 16, position % 16
    x, y = xy // 8 + 2 * (xy // 4 % 2), xy % 4
    z, core = zc // 2, zc % 2
    device = y * 64 + z // 4 * 32 + core * 16 + z % 4 * 4 + x
    r = np.arange(128)
    turn = 2.0 * np.pi / 256
    first = np.concatenate(
        [
            np.cos(turn * (np.outer(r, device) % 256)),
            np.cos(turn * (128 * device % 256))[None],
            -np.sin(turn * (np.outer(r[1:], device) % 256)),
        ]
    )
    m = np.arange(512)
    twist = 2.0 * np.pi / STEPS * np.outer(np.arange(136), m)
    valid = (np.arange(136) <= 128)[:, None]
    twiddle = np.stack([np.cos(twist) * valid, np.sin(twist) * valid]).astype(np.float32)
    even, odd = device[:128], device[128:]
    m = np.arange(256)
    angle_e = 2.0 * np.pi / 512 * (np.outer(np.concatenate([even, 511 - odd]), m) % 512)
    angle_o = 2.0 * np.pi / 512 * (np.outer(np.concatenate([511 - even, odd]), m) % 512)
    second = np.stack([halves(f(a)) for a in (angle_e, angle_o) for f in (np.cos, np.sin)])
    return halves(first), twiddle, second


def split(value):
    high = value.astype(BF16)
    return high, (value - high.astype(F32)).astype(BF16)


def product(a, b, contract):
    def one(left, right):
        return lax.dot_general(left, right, (contract, ((), ())), preferred_element_type=F32)

    return one(a[0], b[0]) + (one(a[0], b[1]) + one(a[1], b[0]))


def exchange_kernel(
    x_hbm, first_hbm, twiddle_hbm, second_hbm, out,
    x_in, first, twiddle, second, send1, mid1, recv1, send2, mid2,
    load_sem, z_send, z_recv, xy_send, xy_recv, own_sem,
):
    y = lax.axis_index("gx")
    gy, gz = lax.axis_index("gy"), lax.axis_index("gz")
    z_hi, core = gy // 2, gy % 2
    z_lo, x = gz // 4, gz % 4
    z = z_hi * 4 + z_lo
    my_zc = z * 2 + core
    my_xy = x % 2 * 8 + x // 2 * 4 + y
    z_peers, xy_peers = [], []
    for dz, dc in Z_ORDER:
        pz = (z + dz + 8) % 8
        pc = 1 - core if dc else core
        z_peers.append((pz * 2 + pc, (y, pz // 4 * 2 + pc, pz % 4 * 4 + x)))
    for dx, dy in XY_ORDER:
        px, py = (x + dx + 4) % 4, (y + dy + 4) % 4
        xy_peers.append((px % 2 * 8 + px // 2 * 4 + py, (py, gy, z_lo * 4 + px)))

    load_x = pltpu.make_async_copy(x_hbm, x_in, load_sem.at[0])
    load_x.start()
    barrier = pltpu.get_barrier_semaphore()
    for _, peer in z_peers + xy_peers:
        pl.semaphore_signal(barrier, inc=1, device_id=peer, device_id_type=MESH)
    loads = [
        pltpu.make_async_copy(source, target, load_sem.at[1 + i])
        for i, (source, target) in enumerate(((first_hbm, first), (twiddle_hbm, twiddle), (second_hbm, second)))
    ]
    for load in loads:
        load.start()

    def over_z(source, target, stage, h, target_outer):
        k = stage * 2 + h
        def place(ref):
            return ref.at[h, my_zc] if target_outer else ref.at[h, :, my_zc]
        for zc, peer in z_peers:
            pltpu.make_async_remote_copy(
                src_ref=source.at[h, :, zc], dst_ref=place(target), send_sem=z_send.at[k], recv_sem=z_recv.at[k],
                device_id=peer, device_id_type=MESH,
            ).start()
        pltpu.make_async_copy(source.at[h, :, my_zc], place(target), own_sem.at[k]).start()

    def over_xy(source, target, stage, h, source_outer):
        k = stage * 2 + h
        def piece(xy):
            return source.at[h, xy] if source_outer else source.at[h, :, xy]
        for xy, peer in xy_peers:
            pltpu.make_async_remote_copy(
                src_ref=piece(xy), dst_ref=target.at[h, my_xy], send_sem=xy_send.at[k], recv_sem=xy_recv.at[k],
                device_id=peer, device_id_type=MESH,
            ).start()
        pltpu.make_async_copy(piece(my_xy), target.at[h, my_xy], own_sem.at[4 + k]).start()

    def wait(target, stage, h, is_z):
        k = stage * 2 + h
        send, recv = (z_send, z_recv) if is_z else (xy_send, xy_recv)
        some = target.at[h, pl.ds(0, 15)]
        pltpu.make_async_copy(some, some, recv.at[k]).wait()
        pltpu.make_async_copy(some, some, send.at[k]).wait()
        one = target.at[h, 0]
        pltpu.make_async_copy(one, one, own_sem.at[k if is_z else 4 + k]).wait()

    flat1 = send1.reshape(2048, 128)
    load_x.wait()
    for h in range(2):
        for k in (2 * h, 2 * h + 1):
            for q in range(4):
                turned = x_in[pl.ds(128 * q, 128), pl.ds(128 * k, 128)].T
                flat1[pl.ds(512 * k + q, 128, stride=4), :] = turned
    pl.semaphore_wait(barrier, 30)

    over_z(send1, mid1, 0, 0, True)
    over_xy(send1, mid1, 0, 1, True)
    for load in loads:
        load.wait()

    def transform(h):
        received = recv1.reshape(2048, 128)
        cos_sin = []
        for side in range(2):
            rows = jnp.concatenate(
                [received[pl.ds(1024 * h + 2 * side + q, 256, stride=4), :] for q in range(2)], axis=1
            )
            mixed = product((first[0], first[1]), split(rows), ((1,), (0,)))
            lanes = pl.ds(256 * side, 256)
            cosine, sine = twiddle[0, :, lanes], twiddle[1, :, lanes]
            re, im = mixed[:128], mixed[128:]
            z_re = re * cosine[:128] + im * sine[:128]
            z_im = im * cosine[:128] - re * sine[:128]
            row = lax.broadcasted_iota(jnp.int32, (128, 256), 0)
            z_im = jnp.where(row == 0, 0.0, z_im)
            h_re = im[:8] * cosine[128:]
            h_im = -im[:8] * sine[128:]
            cos_sin.append((z_re, z_im, h_re, h_im))
        flat2 = send2.reshape(2048, 128)
        lane = lax.broadcasted_iota(jnp.int32, (128, 128), 1)
        for parity in range(2):
            if parity == 0:
                z_re, z_im, h_re, h_im = (a + b for a, b in zip(*cos_sin))
            else:
                z_re, z_im, h_re, h_im = (a - b for a, b in zip(*cos_sin))
            right = split(jnp.concatenate([z_re, z_im], axis=0))
            cosine = (second[2 * parity, 0], second[2 * parity, 1])
            sine = (second[2 * parity + 1, 0], second[2 * parity + 1, 1])
            nt = ((1,), (1,))
            by_cos = product(cosine, right, nt)
            by_sin = product(sine, right, nt)
            out_re = by_cos[:, :128] + by_sin[:, 128:]
            out_im = by_cos[:, 128:] - by_sin[:, :128]
            straight = slice(0, 128) if parity == 0 else slice(128, 256)
            mirror = slice(128, 256) if parity == 0 else slice(0, 128)
            middle_c = split(jnp.concatenate([h_re[:1], h_im[:1], jnp.zeros((126, 256), F32)], axis=0))
            middle_s = split(jnp.concatenate([h_im[:1], -h_re[:1], jnp.zeros((126, 256), F32)], axis=0))
            middle = product(tuple(c[straight] for c in cosine), middle_c, nt)
            middle = middle + product(tuple(s[straight] for s in sine), middle_s, nt)
            base = 1024 * h + 512 * parity
            flat2[pl.ds(base + 0, 128, stride=4), :] = out_re[straight]
            flat2[pl.ds(base + 2, 128, stride=4), :] = out_im[straight]
            mids[parity] = middle
            other = 1024 * h + 512 * (1 - parity)
            mirrors[1 - parity] = (out_re[mirror], -out_im[mirror])
            del other
        for parity in range(2):
            base = 1024 * h + 512 * parity
            m_re, m_im = mirrors[parity]
            middle = mids[parity]
            flat2[pl.ds(base + 1, 128, stride=4), :] = jnp.where(lane == 0, middle, m_re)
            flat2[pl.ds(base + 3, 128, stride=4), :] = jnp.where(lane == 0, pltpu.roll(middle, 127, 1), m_im)

    mids, mirrors = {}, {}

    wait(mid1, 0, 1, False)
    over_z(mid1, recv1, 0, 1, False)
    wait(mid1, 0, 0, True)
    over_xy(mid1, recv1, 0, 0, False)
    wait(recv1, 0, 0, False)
    transform(0)
    over_z(send2, mid2, 1, 0, True)
    wait(recv1, 0, 1, True)
    transform(1)
    over_xy(send2, mid2, 1, 1, True)
    wait(mid2, 1, 1, False)
    over_z(mid2, out, 1, 1, False)
    wait(mid2, 1, 0, True)
    over_xy(mid2, out, 1, 0, False)
    wait(out, 1, 0, False)
    wait(out, 1, 1, True)


def exchange(currents):
    first, twiddle, second = tables()
    buffer = pltpu.VMEM((2, 16, 16, 4, 128), F32)
    anywhere = pl.BlockSpec(memory_space=pl.ANY)
    dma = pltpu.SemaphoreType.DMA
    return pl.pallas_call(
        exchange_kernel,
        out_shape=jax.ShapeDtypeStruct((2, 16, 16, 4, 128), F32),
        in_specs=[anywhere] * 4,
        out_specs=pl.BlockSpec(memory_space=pltpu.VMEM),
        scratch_shapes=[
            pltpu.VMEM((512, 512), F32),
            pltpu.VMEM(first.shape, BF16),
            pltpu.VMEM(twiddle.shape, F32),
            pltpu.VMEM(second.shape, BF16),
            buffer, buffer, buffer, buffer, buffer,
            dma((4,)), dma((4,)), dma((4,)), dma((4,)), dma((4,)), dma((8,)),
        ],
        compiler_params=pltpu.CompilerParams(collective_id=0, has_side_effects=True, vmem_limit_bytes=48 * 1024 * 1024),
        name="exchange",
    )(currents, first, twiddle, second)


def gram_kernel(v, power, cross, high, low, turned_high, turned_low):
    step = pl.program_id(0)

    @pl.when(step == 0)
    def _():
        rows = v.reshape(2048, 128)
        for q in range(4):
            part = rows[pl.ds(q, 512, stride=4), :]
            top, rest = split(part)
            high[:, 128 * q:128 * q + 128] = top
            low[:, 128 * q:128 * q + 128] = rest
            place = 128 * ((q + 2) % 4)
            sign = 1.0 if q >= 2 else -1.0
            turned_high[:, place:place + 128] = (top.astype(F32) * sign).astype(BF16)
            turned_low[:, place:place + 128] = (rest.astype(F32) * sign).astype(BF16)

    nt = ((1,), (1,))
    size = power.shape[0]
    here = pl.ds(pl.multiple_of(step * size, size), size)
    right = (high[...], low[...])
    scaling = 1.0 / (float(STEPS) * 256.0)
    power[...] = product((high[here, :], low[here, :]), right, nt) * scaling
    cross[...] = product((turned_high[here, :], turned_low[here, :]), right, nt) * scaling


def gram(v):
    block = pl.BlockSpec((None, 128, 512), lambda i: (0, i, 0))
    shape = jax.ShapeDtypeStruct((1, 512, 512), F32)
    return pl.pallas_call(
        gram_kernel,
        grid=(4,),
        out_shape=(shape, shape),
        in_specs=[pl.BlockSpec((512, 4, 128), lambda i: (0, 0, 0), pipeline_mode=pl.Buffered(1))],
        out_specs=(block, block),
        scratch_shapes=[pltpu.VMEM((512, 512), BF16)] * 4,
        name="gram",
    )(v)


def on_device(currents):
    return gram(exchange(currents).reshape(512, 4, 128))


def solution(mesh):
    spec = P(AXES, None, None)
    return jax.shard_map(
        on_device, mesh=mesh, in_specs=(P(AXES, None),), out_specs=(spec, spec), check_vma=False
    )
```

```python
import jax
import jax.numpy as jnp
import numpy as np
from jax import lax
from jax.experimental import pallas as pl
from jax.experimental.pallas import tpu as pltpu
from jax.sharding import PartitionSpec as P

MESH = pl.DeviceIdType.MESH
AXES = ("gx", "gy", "gz")
STEPS = 131072
F32, BF16 = jnp.float32, jnp.bfloat16
Z_ORDER = [(d * s, c) for d in (1, 2, 3) for c in (0, 1) for s in (1, -1)] + [(4, 0), (4, 1), (0, 1)]
XY_ORDER = [
    (1, 0), (-1, 0), (0, 1), (0, -1), (1, 1), (-1, -1), (1, -1), (-1, 1),
    (2, 1), (1, 2), (2, -1), (-1, 2), (2, 0), (0, 2), (2, 2),
]


def tables():
    position = np.arange(256)
    xy, zc = position // 16, position % 16
    x, y = xy // 8 + 2 * (xy // 4 % 2), xy % 4
    z, core = zc // 2, zc % 2
    device = y * 64 + z // 4 * 32 + core * 16 + z % 4 * 4 + x
    r = np.arange(128)
    turn = 2.0 * np.pi / 256
    first = np.concatenate(
        [
            np.cos(turn * (np.outer(r, device) % 256)),
            np.cos(turn * (128 * device % 256))[None],
            -np.sin(turn * (np.outer(r[1:], device) % 256)),
        ]
    )
    m = np.arange(512)
    twist = 2.0 * np.pi / STEPS * np.outer(np.arange(136), m)
    valid = (np.arange(136) <= 128)[:, None]
    twiddle = np.stack([np.cos(twist) * valid, np.sin(twist) * valid])
    twiddle = twiddle.reshape(2, 136, 2, 256).transpose(0, 2, 1, 3).reshape(544, 256)
    even, odd = device[:128], device[128:]
    m = np.arange(256)
    angle_e = 2.0 * np.pi / 512 * (np.outer(np.concatenate([even, 511 - odd]), m) % 512)
    angle_o = 2.0 * np.pi / 512 * (np.outer(np.concatenate([511 - even, odd]), m) % 512)
    second = [f(angle) for angle in (angle_e, angle_o) for f in (np.cos, np.sin)]
    return np.concatenate([first, *second, twiddle]).astype(np.float32)


def split(value):
    high = value.astype(BF16)
    return high, (value - high.astype(F32)).astype(BF16)


def product(a, b, contract):
    def one(left, right):
        return lax.dot_general(left, right, (contract, ((), ())), preferred_element_type=F32)

    return one(a[0], b[0]) + (one(a[0], b[1]) + one(a[1], b[0]))


def exchange_kernel(
    x_hbm, table_hbm, power, cross,
    x_in, table, high, low, send1, mid1, recv1, send2, mid2, out, plain, turned_w,
    load_sem, z_send, z_recv, xy_send, xy_recv, own_sem,
):
    y = lax.axis_index("gx")
    gy, gz = lax.axis_index("gy"), lax.axis_index("gz")
    z_hi, core = gy // 2, gy % 2
    z_lo, x = gz // 4, gz % 4
    z = z_hi * 4 + z_lo
    my_zc = z * 2 + core
    my_xy = x % 2 * 8 + x // 2 * 4 + y
    z_peers, xy_peers = [], []
    for dz, dc in Z_ORDER:
        pz = (z + dz + 8) % 8
        pc = 1 - core if dc else core
        z_peers.append((pz * 2 + pc, (y, pz // 4 * 2 + pc, pz % 4 * 4 + x)))
    for dx, dy in XY_ORDER:
        px, py = (x + dx + 4) % 4, (y + dy + 4) % 4
        xy_peers.append((px % 2 * 8 + px // 2 * 4 + py, (py, gy, z_lo * 4 + px)))

    load_x = pltpu.make_async_copy(x_hbm, x_in, load_sem.at[0])
    load_x.start()
    barrier = pltpu.get_barrier_semaphore()
    for _, peer in z_peers + xy_peers:
        pl.semaphore_signal(barrier, inc=1, device_id=peer, device_id_type=MESH)
    load_table = pltpu.make_async_copy(table_hbm, table, load_sem.at[1])
    load_table.start()

    def over_z(source, target, stage, h, target_outer):
        k = stage * 2 + h
        def place(ref):
            return ref.at[h, my_zc] if target_outer else ref.at[h, :, my_zc]
        for zc, peer in z_peers:
            pltpu.make_async_remote_copy(
                src_ref=source.at[h, :, zc], dst_ref=place(target), send_sem=z_send.at[k], recv_sem=z_recv.at[k],
                device_id=peer, device_id_type=MESH,
            ).start()
        pltpu.make_async_copy(source.at[h, :, my_zc], place(target), own_sem.at[k]).start()

    def over_xy(source, target, stage, h, source_outer):
        k = stage * 2 + h
        def piece(xy):
            return source.at[h, xy] if source_outer else source.at[h, :, xy]
        for xy, peer in xy_peers:
            pltpu.make_async_remote_copy(
                src_ref=piece(xy), dst_ref=target.at[h, my_xy], send_sem=xy_send.at[k], recv_sem=xy_recv.at[k],
                device_id=peer, device_id_type=MESH,
            ).start()
        pltpu.make_async_copy(piece(my_xy), target.at[h, my_xy], own_sem.at[4 + k]).start()

    def wait(target, stage, h, is_z):
        k = stage * 2 + h
        send, recv = (z_send, z_recv) if is_z else (xy_send, xy_recv)
        some = target.at[h, pl.ds(0, 15)]
        pltpu.make_async_copy(some, some, recv.at[k]).wait()
        pltpu.make_async_copy(some, some, send.at[k]).wait()
        one = target.at[h, 0]
        pltpu.make_async_copy(one, one, own_sem.at[k if is_z else 4 + k]).wait()

    flat1 = send1.reshape(2048, 128)
    load_x.wait()
    for h in range(2):
        for k in (2 * h, 2 * h + 1):
            for q in range(4):
                turned = x_in[pl.ds(128 * q, 128), pl.ds(128 * k, 128)].T
                flat1[pl.ds(512 * k + q, 128, stride=4), :] = turned
    pl.semaphore_wait(barrier, 30)

    over_z(send1, mid1, 0, 0, True)
    over_xy(send1, mid1, 0, 1, True)
    load_table.wait()
    for i in range(5):
        rows = pl.ds(256 * i, 256)
        high[rows, :], low[rows, :] = split(table[rows, :])

    def matrix(i, start=0, size=256):
        rows = pl.ds(256 * i + start, size)
        return high[rows, :], low[rows, :]

    def transform(h):
        received = recv1.reshape(2048, 128)
        cos_sin = []
        for side in range(2):
            rows = jnp.concatenate(
                [received[pl.ds(1024 * h + 2 * side + q, 256, stride=4), :] for q in range(2)], axis=1
            )
            mixed = product(matrix(0), split(rows), ((1,), (0,)))
            cosine = table[pl.ds(1280 + 136 * side, 136), :]
            sine = table[pl.ds(1552 + 136 * side, 136), :]
            re, im = mixed[:128], mixed[128:]
            z_re = re * cosine[:128] + im * sine[:128]
            z_im = im * cosine[:128] - re * sine[:128]
            row = lax.broadcasted_iota(jnp.int32, (128, 256), 0)
            z_im = jnp.where(row == 0, 0.0, z_im)
            h_re = im[:8] * cosine[128:]
            h_im = -im[:8] * sine[128:]
            cos_sin.append((z_re, z_im, h_re, h_im))
        flat2 = send2.reshape(2048, 128)
        lane = lax.broadcasted_iota(jnp.int32, (128, 128), 1)
        for parity in range(2):
            if parity == 0:
                z_re, z_im, h_re, h_im = (a + b for a, b in zip(*cos_sin))
            else:
                z_re, z_im, h_re, h_im = (a - b for a, b in zip(*cos_sin))
            right = split(jnp.concatenate([z_re, z_im], axis=0))
            nt = ((1,), (1,))
            by_cos = product(matrix(1 + 2 * parity), right, nt)
            by_sin = product(matrix(2 + 2 * parity), right, nt)
            out_re = by_cos[:, :128] + by_sin[:, 128:]
            out_im = by_cos[:, 128:] - by_sin[:, :128]
            straight = slice(0, 128) if parity == 0 else slice(128, 256)
            mirror = slice(128, 256) if parity == 0 else slice(0, 128)
            middle_c = split(jnp.concatenate([h_re[:1], h_im[:1], jnp.zeros((126, 256), F32)], axis=0))
            middle_s = split(jnp.concatenate([h_im[:1], -h_re[:1], jnp.zeros((126, 256), F32)], axis=0))
            middle = product(matrix(1 + 2 * parity, 128 * parity, 128), middle_c, nt)
            middle = middle + product(matrix(2 + 2 * parity, 128 * parity, 128), middle_s, nt)
            base = 1024 * h + 512 * parity
            flat2[pl.ds(base + 0, 128, stride=4), :] = out_re[straight]
            flat2[pl.ds(base + 2, 128, stride=4), :] = out_im[straight]
            mids[parity] = middle
            mirrors[1 - parity] = (out_re[mirror], -out_im[mirror])
        for parity in range(2):
            base = 1024 * h + 512 * parity
            m_re, m_im = mirrors[parity]
            middle = mids[parity]
            flat2[pl.ds(base + 1, 128, stride=4), :] = jnp.where(lane == 0, middle, m_re)
            flat2[pl.ds(base + 3, 128, stride=4), :] = jnp.where(lane == 0, pltpu.roll(middle, 127, 1), m_im)

    mids, mirrors = {}, {}

    wait(mid1, 0, 1, False)
    over_z(mid1, recv1, 0, 1, False)
    wait(mid1, 0, 0, True)
    over_xy(mid1, recv1, 0, 0, False)
    wait(recv1, 0, 0, False)
    transform(0)
    over_z(send2, mid2, 1, 0, True)
    wait(recv1, 0, 1, True)
    transform(1)
    over_xy(send2, mid2, 1, 1, True)
    wait(mid2, 1, 1, False)
    over_z(mid2, out, 1, 1, False)
    wait(mid2, 1, 0, True)
    over_xy(mid2, out, 1, 0, False)
    def spread(h):
        rows = out.reshape(2048, 128)
        here = pl.ds(256 * h, 256)
        for q in range(4):
            high, low = split(rows[pl.ds(1024 * h + q, 256, stride=4), :])
            place = pl.ds(128 * q, 128)
            plain[0, here, place] = high
            plain[1, here, place] = low
            place = pl.ds(128 * ((q + 2) % 4), 128)
            turned_w[0, here, place] = high if q >= 2 else -high
            turned_w[1, here, place] = low if q >= 2 else -low

    nt = ((1,), (1,))
    scaling = 1.0 / (float(STEPS) * 256.0)

    def block(i, j):
        a, b = pl.ds(256 * i, 256), pl.ds(256 * j, 256)
        right = (plain[0, b, :], plain[1, b, :])
        p = product((plain[0, a, :], plain[1, a, :]), right, nt) * scaling
        c = product((turned_w[0, a, :], turned_w[1, a, :]), right, nt) * scaling
        power[0, a, b] = p
        cross[0, a, b] = c
        if i != j:
            power[0, b, a] = p.T
            cross[0, b, a] = -c.T

    wait(out, 1, 0, False)
    spread(0)
    block(0, 0)
    wait(out, 1, 1, True)
    spread(1)
    block(0, 1)
    block(1, 1)


def exchange(currents):
    table = tables()
    buffer = pltpu.VMEM((2, 16, 16, 4, 128), F32)
    anywhere = pl.BlockSpec(memory_space=pl.ANY)
    dma = pltpu.SemaphoreType.DMA
    return pl.pallas_call(
        exchange_kernel,
        out_shape=(jax.ShapeDtypeStruct((1, 512, 512), F32),) * 2,
        in_specs=[anywhere] * 2,
        out_specs=(pl.BlockSpec(memory_space=pltpu.VMEM),) * 2,
        scratch_shapes=[
            pltpu.VMEM((512, 512), F32),
            pltpu.VMEM(table.shape, F32),
            pltpu.VMEM((1280, 256), BF16),
            pltpu.VMEM((1280, 256), BF16),
            buffer, buffer, buffer, buffer, buffer, buffer,
            pltpu.VMEM((2, 512, 512), BF16), pltpu.VMEM((2, 512, 512), BF16),
            dma((2,)), dma((4,)), dma((4,)), dma((4,)), dma((4,)), dma((8,)),
        ],
        compiler_params=pltpu.CompilerParams(collective_id=0, has_side_effects=True, vmem_limit_bytes=51 * 1024 * 1024),
        name="exchange",
    )(currents, table)


def on_device(currents):
    return exchange(currents)


def solution(mesh):
    spec = P(AXES, None, None)
    return jax.shard_map(
        on_device, mesh=mesh, in_specs=(P(AXES, None),), out_specs=(spec, spec), check_vma=False
    )
```

```python
import jax
import jax.numpy as jnp
import numpy as np
from jax import lax
from jax.experimental import pallas as pl
from jax.experimental.pallas import tpu as pltpu
from jax.sharding import PartitionSpec as P

MESH = pl.DeviceIdType.MESH
AXES = ("gx", "gy", "gz")
STEPS = 131072
F32, BF16 = jnp.float32, jnp.bfloat16
Z_ORDER = [(0, 1), (4, 1), (4, 0), (-3, 1), (3, 1), (-3, 0), (3, 0), (-2, 1), (2, 1), (-2, 0), (2, 0), (-1, 1), (1, 1), (-1, 0), (1, 0)]
XY_ORDER = [
    (1, 0), (-1, 0), (0, 1), (0, -1), (1, 1), (-1, -1), (1, -1), (-1, 1),
    (2, 1), (1, 2), (2, -1), (-1, 2), (2, 0), (0, 2), (2, 2),
]
XY_ORDER = XY_ORDER[::-1]


def tables():
    position = np.arange(256)
    xy, zc = position // 16, position % 16
    x, y = xy // 8 + 2 * (xy // 4 % 2), xy % 4
    z, core = zc // 2, zc % 2
    device = y * 64 + z // 4 * 32 + core * 16 + z % 4 * 4 + x
    r = np.arange(128)
    turn = 2.0 * np.pi / 256
    first = np.concatenate(
        [
            np.cos(turn * (np.outer(r, device) % 256)),
            np.cos(turn * (128 * device % 256))[None],
            -np.sin(turn * (np.outer(r[1:], device) % 256)),
        ]
    )
    m = np.arange(512)
    twist = 2.0 * np.pi / STEPS * np.outer(np.arange(136), m)
    valid = (np.arange(136) <= 128)[:, None]
    twiddle = np.stack([np.cos(twist) * valid, np.sin(twist) * valid])
    twiddle = twiddle.reshape(2, 136, 2, 256).transpose(0, 2, 1, 3).reshape(544, 256)
    even, odd = device[:128], device[128:]
    m = np.arange(256)
    angle_e = 2.0 * np.pi / 512 * (np.outer(np.concatenate([even, 511 - odd]), m) % 512)
    angle_o = 2.0 * np.pi / 512 * (np.outer(np.concatenate([511 - even, odd]), m) % 512)
    second = [f(angle) for angle in (angle_e, angle_o) for f in (np.cos, np.sin)]
    return np.concatenate([first, *second, twiddle]).astype(np.float32)


def split(value):
    high = value.astype(BF16)
    return high, (value - high.astype(F32)).astype(BF16)


def product(a, b, contract):
    def one(left, right):
        return lax.dot_general(left, right, (contract, ((), ())), preferred_element_type=F32)

    return one(a[0], b[0]) + (one(a[0], b[1]) + one(a[1], b[0]))


def exchange_kernel(
    x_hbm, table_hbm, power, cross,
    x_in, table, high, low, send1, mid1, recv1, send2, mid2, out, plain, turned_w,
    load_sem, z_send, z_recv, xy_send, xy_recv, own_sem,
):
    y = lax.axis_index("gx")
    gy, gz = lax.axis_index("gy"), lax.axis_index("gz")
    z_hi, core = gy // 2, gy % 2
    z_lo, x = gz // 4, gz % 4
    z = z_hi * 4 + z_lo
    my_zc = z * 2 + core
    my_xy = x % 2 * 8 + x // 2 * 4 + y
    z_peers, xy_peers = [], []
    for dz, dc in Z_ORDER:
        pz = (z + dz + 8) % 8
        pc = 1 - core if dc else core
        z_peers.append((pz * 2 + pc, (y, pz // 4 * 2 + pc, pz % 4 * 4 + x)))
    for dx, dy in XY_ORDER:
        px, py = (x + dx + 4) % 4, (y + dy + 4) % 4
        xy_peers.append((px % 2 * 8 + px // 2 * 4 + py, (py, gy, z_lo * 4 + px)))

    load_x = pltpu.make_async_copy(x_hbm, x_in, load_sem.at[0])
    load_x.start()
    barrier = pltpu.get_barrier_semaphore()
    for _, peer in z_peers + xy_peers:
        pl.semaphore_signal(barrier, inc=1, device_id=peer, device_id_type=MESH)
    load_table = pltpu.make_async_copy(table_hbm, table, load_sem.at[1])
    load_table.start()

    def over_z(source, target, stage, h, target_outer):
        k = stage * 2 + h
        def place(ref):
            return ref.at[h, my_zc] if target_outer else ref.at[h, :, my_zc]
        for zc, peer in z_peers:
            pltpu.make_async_remote_copy(
                src_ref=source.at[h, :, zc], dst_ref=place(target), send_sem=z_send.at[k], recv_sem=z_recv.at[k],
                device_id=peer, device_id_type=MESH,
            ).start()
        pltpu.make_async_copy(source.at[h, :, my_zc], place(target), own_sem.at[k]).start()

    def over_xy(source, target, stage, h, source_outer):
        k = stage * 2 + h
        def piece(xy):
            return source.at[h, xy] if source_outer else source.at[h, :, xy]
        for xy, peer in xy_peers:
            pltpu.make_async_remote_copy(
                src_ref=piece(xy), dst_ref=target.at[h, my_xy], send_sem=xy_send.at[k], recv_sem=xy_recv.at[k],
                device_id=peer, device_id_type=MESH,
            ).start()
        pltpu.make_async_copy(piece(my_xy), target.at[h, my_xy], own_sem.at[4 + k]).start()

    def wait(target, stage, h, is_z):
        k = stage * 2 + h
        send, recv = (z_send, z_recv) if is_z else (xy_send, xy_recv)
        some = target.at[h, pl.ds(0, 15)]
        pltpu.make_async_copy(some, some, recv.at[k]).wait()
        pltpu.make_async_copy(some, some, send.at[k]).wait()
        one = target.at[h, 0]
        pltpu.make_async_copy(one, one, own_sem.at[k if is_z else 4 + k]).wait()

    flat1 = send1.reshape(2048, 128)
    load_x.wait()
    for h in range(2):
        for k in (2 * h, 2 * h + 1):
            for q in range(4):
                turned = x_in[pl.ds(128 * q, 128), pl.ds(128 * k, 128)].T
                flat1[pl.ds(512 * k + q, 128, stride=4), :] = turned
    pl.semaphore_wait(barrier, 30)

    over_z(send1, mid1, 0, 0, True)
    over_xy(send1, mid1, 0, 1, True)
    load_table.wait()
    for i in range(5):
        rows = pl.ds(256 * i, 256)
        high[rows, :], low[rows, :] = split(table[rows, :])

    def matrix(i, start=0, size=256):
        rows = pl.ds(256 * i + start, size)
        return high[rows, :], low[rows, :]

    def transform(h):
        received = recv1.reshape(2048, 128)
        cos_sin = []
        for side in range(2):
            rows = jnp.concatenate(
                [received[pl.ds(1024 * h + 2 * side + q, 256, stride=4), :] for q in range(2)], axis=1
            )
            mixed = product(matrix(0), split(rows), ((1,), (0,)))
            cosine = table[pl.ds(1280 + 136 * side, 136), :]
            sine = table[pl.ds(1552 + 136 * side, 136), :]
            re, im = mixed[:128], mixed[128:]
            z_re = re * cosine[:128] + im * sine[:128]
            z_im = im * cosine[:128] - re * sine[:128]
            row = lax.broadcasted_iota(jnp.int32, (128, 256), 0)
            z_im = jnp.where(row == 0, 0.0, z_im)
            h_re = im[:8] * cosine[128:]
            h_im = -im[:8] * sine[128:]
            cos_sin.append((z_re, z_im, h_re, h_im))
        flat2 = send2.reshape(2048, 128)
        lane = lax.broadcasted_iota(jnp.int32, (128, 128), 1)
        for parity in range(2):
            if parity == 0:
                z_re, z_im, h_re, h_im = (a + b for a, b in zip(*cos_sin))
            else:
                z_re, z_im, h_re, h_im = (a - b for a, b in zip(*cos_sin))
            right = split(jnp.concatenate([z_re, z_im], axis=0))
            nt = ((1,), (1,))
            by_cos = product(matrix(1 + 2 * parity), right, nt)
            by_sin = product(matrix(2 + 2 * parity), right, nt)
            out_re = by_cos[:, :128] + by_sin[:, 128:]
            out_im = by_cos[:, 128:] - by_sin[:, :128]
            straight = slice(0, 128) if parity == 0 else slice(128, 256)
            mirror = slice(128, 256) if parity == 0 else slice(0, 128)
            middle_c = split(jnp.concatenate([h_re[:1], h_im[:1], jnp.zeros((126, 256), F32)], axis=0))
            middle_s = split(jnp.concatenate([h_im[:1], -h_re[:1], jnp.zeros((126, 256), F32)], axis=0))
            middle = product(matrix(1 + 2 * parity, 128 * parity, 128), middle_c, nt)
            middle = middle + product(matrix(2 + 2 * parity, 128 * parity, 128), middle_s, nt)
            base = 1024 * h + 512 * parity
            flat2[pl.ds(base + 0, 128, stride=4), :] = out_re[straight]
            flat2[pl.ds(base + 2, 128, stride=4), :] = out_im[straight]
            mids[parity] = middle
            mirrors[1 - parity] = (out_re[mirror], -out_im[mirror])
        for parity in range(2):
            base = 1024 * h + 512 * parity
            m_re, m_im = mirrors[parity]
            middle = mids[parity]
            flat2[pl.ds(base + 1, 128, stride=4), :] = jnp.where(lane == 0, middle, m_re)
            flat2[pl.ds(base + 3, 128, stride=4), :] = jnp.where(lane == 0, pltpu.roll(middle, 127, 1), m_im)

    mids, mirrors = {}, {}

    wait(mid1, 0, 1, False)
    over_z(mid1, recv1, 0, 1, False)
    wait(mid1, 0, 0, True)
    over_xy(mid1, recv1, 0, 0, False)
    wait(recv1, 0, 0, False)
    transform(0)
    over_z(send2, mid2, 1, 0, True)
    wait(recv1, 0, 1, True)
    transform(1)
    over_xy(send2, mid2, 1, 1, True)
    wait(mid2, 1, 1, False)
    over_z(mid2, out, 1, 1, False)
    wait(mid2, 1, 0, True)
    over_xy(mid2, out, 1, 0, False)
    def spread(h):
        rows = out.reshape(2048, 128)
        here = pl.ds(256 * h, 256)
        for q in range(4):
            high, low = split(rows[pl.ds(1024 * h + q, 256, stride=4), :])
            place = pl.ds(128 * q, 128)
            plain[0, here, place] = high
            plain[1, here, place] = low
            place = pl.ds(128 * ((q + 2) % 4), 128)
            turned_w[0, here, place] = high if q >= 2 else -high
            turned_w[1, here, place] = low if q >= 2 else -low

    nt = ((1,), (1,))
    scaling = 1.0 / (float(STEPS) * 256.0)

    def block(i, j):
        a, b = pl.ds(256 * i, 256), pl.ds(256 * j, 256)
        right = (plain[0, b, :], plain[1, b, :])
        p = product((plain[0, a, :], plain[1, a, :]), right, nt) * scaling
        c = product((turned_w[0, a, :], turned_w[1, a, :]), right, nt) * scaling
        power[0, a, b] = p
        cross[0, a, b] = c
        if i != j:
            power[0, b, a] = p.T
            cross[0, b, a] = -c.T

    wait(out, 1, 0, False)
    spread(0)
    block(0, 0)
    wait(out, 1, 1, True)
    spread(1)
    block(0, 1)
    block(1, 1)


def exchange(currents):
    table = tables()
    buffer = pltpu.VMEM((2, 16, 16, 4, 128), F32)
    anywhere = pl.BlockSpec(memory_space=pl.ANY)
    dma = pltpu.SemaphoreType.DMA
    return pl.pallas_call(
        exchange_kernel,
        out_shape=(jax.ShapeDtypeStruct((1, 512, 512), F32),) * 2,
        in_specs=[anywhere] * 2,
        out_specs=(pl.BlockSpec(memory_space=pltpu.VMEM),) * 2,
        scratch_shapes=[
            pltpu.VMEM((512, 512), F32),
            pltpu.VMEM(table.shape, F32),
            pltpu.VMEM((1280, 256), BF16),
            pltpu.VMEM((1280, 256), BF16),
            buffer, buffer, buffer, buffer, buffer, buffer,
            pltpu.VMEM((2, 512, 512), BF16), pltpu.VMEM((2, 512, 512), BF16),
            dma((2,)), dma((4,)), dma((4,)), dma((4,)), dma((4,)), dma((8,)),
        ],
        compiler_params=pltpu.CompilerParams(collective_id=0, has_side_effects=True, vmem_limit_bytes=51 * 1024 * 1024),
        name="exchange",
    )(currents, table)


def on_device(currents):
    return exchange(currents)


def solution(mesh):
    spec = P(AXES, None, None)
    return jax.shard_map(
        on_device, mesh=mesh, in_specs=(P(AXES, None),), out_specs=(spec, spec), check_vma=False
    )
```

```python
import functools

import jax
import jax.numpy as jnp
import numpy as np
from jax import lax
from jax.experimental import pallas as pl
from jax.experimental.pallas import tpu as pltpu
from jax.sharding import PartitionSpec as P

MESH = pl.DeviceIdType.MESH
AXES = ("gx", "gy", "gz")
STEPS = 131072
F32, BF16 = jnp.float32, jnp.bfloat16
Z_ORDER = [(0, 1), (4, 1), (4, 0), (-3, 1), (3, 1), (-3, 0), (3, 0), (-2, 1), (2, 1), (-2, 0), (2, 0), (-1, 1), (1, 1), (-1, 0), (1, 0)]
XY_ORDER = [
    (1, 0), (-1, 0), (0, 1), (0, -1), (1, 1), (-1, -1), (1, -1), (-1, 1),
    (2, 1), (1, 2), (2, -1), (-1, 2), (2, 0), (0, 2), (2, 2),
]
XY_ORDER = XY_ORDER[::-1]


def tables():
    position = np.arange(256)
    xy, zc = position // 16, position % 16
    x, y = xy // 8 + 2 * (xy // 4 % 2), xy % 4
    z, core = zc // 2, zc % 2
    device = y * 64 + z // 4 * 32 + core * 16 + z % 4 * 4 + x
    r = np.arange(128)
    turn = 2.0 * np.pi / 256
    first = np.concatenate(
        [
            np.cos(turn * (np.outer(r, device) % 256)),
            np.cos(turn * (128 * device % 256))[None],
            -np.sin(turn * (np.outer(r[1:], device) % 256)),
        ]
    )
    m = np.arange(512)
    twist = 2.0 * np.pi / STEPS * np.outer(np.arange(136), m)
    valid = (np.arange(136) <= 128)[:, None]
    twiddle = np.stack([np.cos(twist) * valid, np.sin(twist) * valid])
    twiddle = twiddle.reshape(2, 136, 2, 256).transpose(0, 2, 1, 3).reshape(544, 256)
    even, odd = device[:128], device[128:]
    m = np.arange(256)
    angle_e = 2.0 * np.pi / 512 * (np.outer(np.concatenate([even, 511 - odd]), m) % 512)
    angle_o = 2.0 * np.pi / 512 * (np.outer(np.concatenate([511 - even, odd]), m) % 512)
    second = [f(angle) for angle in (angle_e, angle_o) for f in (np.cos, np.sin)]
    return np.concatenate([first, *second, twiddle]).astype(np.float32)


def split(value):
    high = value.astype(BF16)
    return high, (value - high.astype(F32)).astype(BF16)


def product(a, b, contract):
    def one(left, right):
        return lax.dot_general(left, right, (contract, ((), ())), preferred_element_type=F32)

    return one(a[0], b[0]) + (one(a[0], b[1]) + one(a[1], b[0]))


SCALING = 1.0 / (float(STEPS) * 256.0)
NT = ((1,), (1,))
BOTH, RE, IM = pl.ds(0, 512), pl.ds(0, 256), pl.ds(256, 256)


def modes_of(plain, block, lanes):
    rows = pl.ds(256 * block, 256)
    return plain[0, rows, lanes], plain[1, rows, lanes]


def power_block(plain, i, j):
    return product(modes_of(plain, i, BOTH), modes_of(plain, j, BOTH), NT) * SCALING


def cross_block(plain, i, j):
    cross = product(modes_of(plain, i, IM), modes_of(plain, j, RE), NT)
    other = cross.T if i == j else product(modes_of(plain, i, RE), modes_of(plain, j, IM), NT)
    return (cross - other) * SCALING


def exchange_kernel(
    x_hbm, table_hbm, power, cross, plain,
    x_in, table, high, low, send1, mid1, recv1, send2, mid2, out,
    load_sem, z_send, z_recv, xy_send, xy_recv, own_sem,
):
    load_x = []
    for h in range(2):
        columns = pl.ds(256 * h, 256)
        load_x.append(pltpu.make_async_copy(x_hbm.at[:, columns], x_in.at[:, columns], load_sem.at[h]))
        load_x[h].start()
    y = lax.axis_index("gx")
    gy, gz = lax.axis_index("gy"), lax.axis_index("gz")
    z_hi, core = gy // 2, gy % 2
    z_lo, x = gz // 4, gz % 4
    z = z_hi * 4 + z_lo
    my_zc = z * 2 + core
    my_xy = x % 2 * 8 + x // 2 * 4 + y
    z_peers, xy_peers = [], []
    for dz, dc in Z_ORDER:
        pz = (z + dz + 8) % 8
        pc = 1 - core if dc else core
        z_peers.append((pz * 2 + pc, (y, pz // 4 * 2 + pc, pz % 4 * 4 + x)))
    for dx, dy in XY_ORDER:
        px, py = (x + dx + 4) % 4, (y + dy + 4) % 4
        xy_peers.append((px % 2 * 8 + px // 2 * 4 + py, (py, gy, z_lo * 4 + px)))

    barrier = pltpu.get_barrier_semaphore()
    for _, peer in z_peers + xy_peers:
        pl.semaphore_signal(barrier, inc=1, device_id=peer, device_id_type=MESH)
    load_table = pltpu.make_async_copy(table_hbm, table, load_sem.at[2])
    load_table.start()

    def over_z(source, target, stage, h, target_outer):
        k = stage * 2 + h
        def place(ref):
            return ref.at[h, my_zc] if target_outer else ref.at[h, :, my_zc]
        def send(zc, peer):
            pltpu.make_async_remote_copy(
                src_ref=source.at[h, :, zc], dst_ref=place(target), send_sem=z_send.at[k], recv_sem=z_recv.at[k],
                device_id=peer, device_id_type=MESH,
            ).start()

        if k == 3:
            for pz in (0, 1, 2, 3, 7, 6, 4, 5):
                for pc in (1 - core, core):
                    zc = pz * 2 + pc
                    pl.when(zc != my_zc)(functools.partial(send, zc, (y, pz // 4 * 2 + pc, pz % 4 * 4 + x)))
        else:
            for zc, peer in z_peers:
                send(zc, peer)
        pltpu.make_async_copy(source.at[h, :, my_zc], place(target), own_sem.at[k]).start()

    def over_xy(source, target, stage, h, source_outer):
        k = stage * 2 + h
        def piece(xy):
            return source.at[h, xy] if source_outer else source.at[h, :, xy]
        for xy, peer in xy_peers:
            pltpu.make_async_remote_copy(
                src_ref=piece(xy), dst_ref=target.at[h, my_xy], send_sem=xy_send.at[k], recv_sem=xy_recv.at[k],
                device_id=peer, device_id_type=MESH,
            ).start()
        pltpu.make_async_copy(piece(my_xy), target.at[h, my_xy], own_sem.at[4 + k]).start()

    def wait(target, stage, h, is_z):
        k = stage * 2 + h
        send, recv = (z_send, z_recv) if is_z else (xy_send, xy_recv)
        some = target.at[h, pl.ds(0, 15)]
        pltpu.make_async_copy(some, some, recv.at[k]).wait()
        pltpu.make_async_copy(some, some, send.at[k]).wait()
        one = target.at[h, 0]
        pltpu.make_async_copy(one, one, own_sem.at[k if is_z else 4 + k]).wait()

    flat1 = send1.reshape(2048, 128)
    def turn(h):
        load_x[h].wait()
        for k in (2 * h, 2 * h + 1):
            for q in range(4):
                turned = x_in[pl.ds(128 * q, 128), pl.ds(128 * k, 128)].T
                flat1[pl.ds(512 * k + q, 128, stride=4), :] = turned

    turn(0)
    pl.semaphore_wait(barrier, 30)
    over_z(send1, mid1, 0, 0, True)
    turn(1)
    over_xy(send1, mid1, 0, 1, True)
    load_table.wait()
    for i in range(5):
        rows = pl.ds(256 * i, 256)
        high[rows, :], low[rows, :] = split(table[rows, :])

    def matrix(i, start=0, size=256):
        rows = pl.ds(256 * i + start, size)
        return high[rows, :], low[rows, :]

    def transform(h):
        received = recv1.reshape(2048, 128)
        cos_sin = []
        for side in range(2):
            rows = jnp.concatenate(
                [received[pl.ds(1024 * h + 2 * side + q, 256, stride=4), :] for q in range(2)], axis=1
            )
            mixed = product(matrix(0), split(rows), ((1,), (0,)))
            cosine = table[pl.ds(1280 + 136 * side, 136), :]
            sine = table[pl.ds(1552 + 136 * side, 136), :]
            re, im = mixed[:128], mixed[128:]
            z_re = re * cosine[:128] + im * sine[:128]
            z_im = im * cosine[:128] - re * sine[:128]
            row = lax.broadcasted_iota(jnp.int32, (128, 256), 0)
            z_im = jnp.where(row == 0, 0.0, z_im)
            h_re = im[:8] * cosine[128:]
            h_im = -im[:8] * sine[128:]
            cos_sin.append((z_re, z_im, h_re, h_im))
        flat2 = send2.reshape(2048, 128)
        lane = lax.broadcasted_iota(jnp.int32, (128, 128), 1)
        for parity in range(2):
            if parity == 0:
                z_re, z_im, h_re, h_im = (a + b for a, b in zip(*cos_sin))
            else:
                z_re, z_im, h_re, h_im = (a - b for a, b in zip(*cos_sin))
            right = split(jnp.concatenate([z_re, z_im], axis=0))
            nt = ((1,), (1,))
            by_cos = product(matrix(1 + 2 * parity), right, nt)
            by_sin = product(matrix(2 + 2 * parity), right, nt)
            out_re = by_cos[:, :128] + by_sin[:, 128:]
            out_im = by_cos[:, 128:] - by_sin[:, :128]
            straight = slice(0, 128) if parity == 0 else slice(128, 256)
            mirror = slice(128, 256) if parity == 0 else slice(0, 128)
            middle_c = split(jnp.concatenate([h_re[:1], h_im[:1], jnp.zeros((126, 256), F32)], axis=0))
            middle_s = split(jnp.concatenate([h_im[:1], -h_re[:1], jnp.zeros((126, 256), F32)], axis=0))
            middle = product(matrix(1 + 2 * parity, 128 * parity, 128), middle_c, nt)
            middle = middle + product(matrix(2 + 2 * parity, 128 * parity, 128), middle_s, nt)
            base = 1024 * h + 512 * parity
            flat2[pl.ds(base + 0, 128, stride=4), :] = out_re[straight]
            flat2[pl.ds(base + 2, 128, stride=4), :] = out_im[straight]
            mids[parity] = middle
            mirrors[1 - parity] = (out_re[mirror], -out_im[mirror])
        for parity in range(2):
            base = 1024 * h + 512 * parity
            m_re, m_im = mirrors[parity]
            middle = mids[parity]
            flat2[pl.ds(base + 1, 128, stride=4), :] = jnp.where(lane == 0, middle, m_re)
            flat2[pl.ds(base + 3, 128, stride=4), :] = jnp.where(lane == 0, pltpu.roll(middle, 127, 1), m_im)

    mids, mirrors = {}, {}

    wait(mid1, 0, 1, False)
    over_z(mid1, recv1, 0, 1, False)
    wait(mid1, 0, 0, True)
    over_xy(mid1, recv1, 0, 0, False)
    wait(recv1, 0, 0, False)
    transform(0)
    over_z(send2, mid2, 1, 0, True)
    wait(recv1, 0, 1, True)
    transform(1)
    over_xy(send2, mid2, 1, 1, True)
    wait(mid2, 1, 1, False)
    over_z(mid2, out, 1, 1, False)
    wait(mid2, 1, 0, True)
    over_xy(mid2, out, 1, 0, False)
    def spread(h):
        rows = out.reshape(2048, 128)
        here = pl.ds(256 * h, 256)
        for q in range(4):
            high, low = split(rows[pl.ds(1024 * h + q, 256, stride=4), :])
            place = pl.ds(128 * q, 128)
            plain[0, here, place] = high
            plain[1, here, place] = low

    wait(out, 1, 0, False)
    spread(0)
    power[...] = power_block(plain, 0, 0)
    cross[...] = cross_block(plain, 0, 0)
    wait(out, 1, 1, True)
    spread(1)


def exchange(currents):
    table = tables()
    buffer = pltpu.VMEM((2, 16, 16, 4, 128), F32)
    anywhere = pl.BlockSpec(memory_space=pl.ANY)
    dma = pltpu.SemaphoreType.DMA
    return pl.pallas_call(
        exchange_kernel,
        out_shape=(jax.ShapeDtypeStruct((256, 256), F32),) * 2 + (jax.ShapeDtypeStruct((2, 512, 512), BF16),),
        in_specs=[anywhere] * 2,
        out_specs=(pl.BlockSpec(memory_space=pltpu.VMEM),) * 3,
        scratch_shapes=[
            pltpu.VMEM((512, 512), F32),
            pltpu.VMEM(table.shape, F32),
            pltpu.VMEM((1280, 256), BF16),
            pltpu.VMEM((1280, 256), BF16),
            buffer, buffer, buffer, buffer, buffer, buffer,
            dma((3,)), dma((4,)), dma((4,)), dma((4,)), dma((4,)), dma((8,)),
        ],
        compiler_params=pltpu.CompilerParams(collective_id=0, has_side_effects=True, vmem_limit_bytes=54001664),
        name="exchange",
    )(currents, table)


def finish_kernel(power00, cross00, plain, power, cross, blocks, sem):
    copies = []

    def put(source, target, i, j):
        place = target.at[0, pl.ds(256 * i, 256), pl.ds(256 * j, 256)]
        copies.append(pltpu.make_async_copy(source, place, sem.at[len(copies)]))
        copies[-1].start()

    put(power00, power, 0, 0)
    put(cross00, cross, 0, 0)
    blocks[0] = power_block(plain, 0, 1)
    put(blocks.at[0], power, 0, 1)
    blocks[1] = blocks[0].T
    put(blocks.at[1], power, 1, 0)
    blocks[2] = cross_block(plain, 0, 1)
    put(blocks.at[2], cross, 0, 1)
    blocks[3] = -blocks[2].T
    put(blocks.at[3], cross, 1, 0)
    blocks[4] = power_block(plain, 1, 1)
    put(blocks.at[4], power, 1, 1)
    blocks[5] = cross_block(plain, 1, 1)
    put(blocks.at[5], cross, 1, 1)
    for copy in copies:
        copy.wait()


def on_device(currents):
    here = pl.BlockSpec(memory_space=pltpu.VMEM)
    shape = jax.ShapeDtypeStruct((1, 512, 512), F32)
    return pl.pallas_call(
        finish_kernel,
        out_shape=(shape, shape),
        in_specs=[here] * 3,
        out_specs=(pl.BlockSpec(memory_space=pltpu.HBM),) * 2,
        scratch_shapes=[pltpu.VMEM((6, 256, 256), F32), pltpu.SemaphoreType.DMA((8,))],
        compiler_params=pltpu.CompilerParams(vmem_limit_bytes=8 * 1024 * 1024),
        name="finish",
    )(*exchange(currents))


def solution(mesh):
    spec = P(AXES, None, None)
    return jax.shard_map(
        on_device, mesh=mesh, in_specs=(P(AXES, None),), out_specs=(spec, spec), check_vma=False
    )
```

```python
import functools

import jax
import jax.numpy as jnp
import numpy as np
from jax import lax
from jax.experimental import pallas as pl
from jax.experimental.pallas import tpu as pltpu
from jax.sharding import PartitionSpec as P

MESH = pl.DeviceIdType.MESH
AXES = ("gx", "gy", "gz")
STEPS = 131072
F32, BF16 = jnp.float32, jnp.bfloat16
Z_ORDER = [(0, 1), (4, 1), (4, 0), (-3, 1), (3, 1), (-3, 0), (3, 0), (-2, 1), (2, 1), (-2, 0), (2, 0), (-1, 1), (1, 1), (-1, 0), (1, 0)]
XY_ORDER = [
    (1, 0), (-1, 0), (0, 1), (0, -1), (1, 1), (-1, -1), (1, -1), (-1, 1),
    (2, 1), (1, 2), (2, -1), (-1, 2), (2, 0), (0, 2), (2, 2),
]
XY_ORDER = XY_ORDER[::-1]


def tables():
    position = np.arange(256)
    xy, zc = position // 16, position % 16
    x, y = xy // 8 + 2 * (xy // 4 % 2), xy % 4
    z, core = zc // 2, zc % 2
    device = y * 64 + z // 4 * 32 + core * 16 + z % 4 * 4 + x
    r = np.arange(128)
    turn = 2.0 * np.pi / 256
    first = np.concatenate(
        [
            np.cos(turn * (np.outer(r, device) % 256)),
            np.cos(turn * (128 * device % 256))[None],
            -np.sin(turn * (np.outer(r[1:], device) % 256)),
        ]
    )
    m = np.arange(512)
    twist = 2.0 * np.pi / STEPS * np.outer(np.arange(136), m)
    valid = (np.arange(136) <= 128)[:, None]
    twiddle = np.stack([np.cos(twist) * valid, np.sin(twist) * valid])
    twiddle = twiddle.reshape(2, 136, 2, 256).transpose(0, 2, 1, 3).reshape(544, 256)
    even, odd = device[:128], device[128:]
    m = np.arange(256)
    angle_e = 2.0 * np.pi / 512 * (np.outer(np.concatenate([even, 511 - odd]), m) % 512)
    angle_o = 2.0 * np.pi / 512 * (np.outer(np.concatenate([511 - even, odd]), m) % 512)
    second = [f(angle) for angle in (angle_e, angle_o) for f in (np.cos, np.sin)]
    return np.concatenate([first, *second, twiddle]).astype(np.float32)


def split(value):
    high = value.astype(BF16)
    return high, (value - high.astype(F32)).astype(BF16)


def product(a, b, contract):
    def one(left, right):
        return lax.dot_general(left, right, (contract, ((), ())), preferred_element_type=F32)

    return one(a[0], b[0]) + (one(a[0], b[1]) + one(a[1], b[0]))


SCALING = 1.0 / (float(STEPS) * 256.0)
NT = ((1,), (1,))
BOTH, RE, IM = pl.ds(0, 512), pl.ds(0, 256), pl.ds(256, 256)


def modes_of(plain, block, lanes):
    rows = pl.ds(256 * block, 256)
    return plain[0, rows, lanes], plain[1, rows, lanes]


def power_block(plain, i, j):
    return product(modes_of(plain, i, BOTH), modes_of(plain, j, BOTH), NT) * SCALING


def cross_block(plain, i, j):
    cross = product(modes_of(plain, i, IM), modes_of(plain, j, RE), NT)
    other = cross.T if i == j else product(modes_of(plain, i, RE), modes_of(plain, j, IM), NT)
    return (cross - other) * SCALING


def exchange_kernel(
    x_hbm, table_hbm, power, cross, plain,
    x_in, table, high, low, send1, mid1, recv1, send2, mid2, out,
    load_sem, z_send, z_recv, xy_send, xy_recv, own_sem,
):
    load_x = []
    for h in range(2):
        columns = pl.ds(256 * h, 256)
        load_x.append(pltpu.make_async_copy(x_hbm.at[:, columns], x_in.at[:, columns], load_sem.at[h]))
        load_x[h].start()
    y = lax.axis_index("gx")
    gy, gz = lax.axis_index("gy"), lax.axis_index("gz")
    z_hi, core = gy // 2, gy % 2
    z_lo, x = gz // 4, gz % 4
    z = z_hi * 4 + z_lo
    my_zc = z * 2 + core
    my_xy = x % 2 * 8 + x // 2 * 4 + y
    z_peers, xy_peers = [], []
    way = 1 - 2 * core
    for dz, dc in Z_ORDER:
        pz = (z + dz * way + 8) % 8
        pc = 1 - core if dc else core
        z_peers.append((pz * 2 + pc, (y, pz // 4 * 2 + pc, pz % 4 * 4 + x)))
    for dx, dy in XY_ORDER:
        px, py = (x + dx * way + 4) % 4, (y + dy * way + 4) % 4
        xy_peers.append((px % 2 * 8 + px // 2 * 4 + py, (py, gy, z_lo * 4 + px)))

    barrier = pltpu.get_barrier_semaphore()
    for _, peer in z_peers + xy_peers:
        pl.semaphore_signal(barrier, inc=1, device_id=peer, device_id_type=MESH)
    load_table = pltpu.make_async_copy(table_hbm, table, load_sem.at[2])
    load_table.start()

    def over_z(source, target, stage, h, target_outer):
        k = stage * 2 + h
        def place(ref):
            return ref.at[h, my_zc] if target_outer else ref.at[h, :, my_zc]
        def send(zc, peer):
            pltpu.make_async_remote_copy(
                src_ref=source.at[h, :, zc], dst_ref=place(target), send_sem=z_send.at[k], recv_sem=z_recv.at[k],
                device_id=peer, device_id_type=MESH,
            ).start()

        if k >= 2:
            for pz in ((0, 1, 2, 7, 3, 6, 4, 5) if h else (0, 1, 2, 3, 7, 6, 4, 5)):
                for pc in (1 - core, core):
                    zc = pz * 2 + pc
                    pl.when(zc != my_zc)(functools.partial(send, zc, (y, pz // 4 * 2 + pc, pz % 4 * 4 + x)))
        else:
            for zc, peer in z_peers:
                send(zc, peer)
        pltpu.make_async_copy(source.at[h, :, my_zc], place(target), own_sem.at[k]).start()

    def over_xy(source, target, stage, h, source_outer):
        k = stage * 2 + h
        def piece(xy):
            return source.at[h, xy] if source_outer else source.at[h, :, xy]
        for xy, peer in xy_peers:
            pltpu.make_async_remote_copy(
                src_ref=piece(xy), dst_ref=target.at[h, my_xy], send_sem=xy_send.at[k], recv_sem=xy_recv.at[k],
                device_id=peer, device_id_type=MESH,
            ).start()
        pltpu.make_async_copy(piece(my_xy), target.at[h, my_xy], own_sem.at[4 + k]).start()

    def wait(target, stage, h, is_z):
        k = stage * 2 + h
        some = target.at[h, pl.ds(0, 15)]
        pltpu.make_async_copy(some, some, (z_recv if is_z else xy_recv).at[k]).wait()
        one = target.at[h, 0]
        pltpu.make_async_copy(one, one, own_sem.at[k if is_z else 4 + k]).wait()

    def drain():
        for k in range(4):
            for sem in (z_send, xy_send):
                some = mid1.at[0, pl.ds(0, 15)]
                pltpu.make_async_copy(some, some, sem.at[k]).wait()

    flat1 = send1.reshape(2048, 128)
    def turn(h):
        load_x[h].wait()
        for k in (2 * h, 2 * h + 1):
            for q in range(4):
                turned = x_in[pl.ds(128 * q, 128), pl.ds(128 * k, 128)].T
                flat1[pl.ds(512 * k + q, 128, stride=4), :] = turned

    turn(0)
    pl.semaphore_wait(barrier, 30)
    over_z(send1, mid1, 0, 0, True)
    turn(1)
    over_xy(send1, mid1, 0, 1, True)
    load_table.wait()
    for i in range(5):
        rows = pl.ds(256 * i, 256)
        high[rows, :], low[rows, :] = split(table[rows, :])

    def matrix(i, start=0, size=256):
        rows = pl.ds(256 * i + start, size)
        return high[rows, :], low[rows, :]

    def transform(h):
        received = recv1.reshape(2048, 128)
        cos_sin = []
        for side in range(2):
            rows = jnp.concatenate(
                [received[pl.ds(1024 * h + 2 * side + q, 256, stride=4), :] for q in range(2)], axis=1
            )
            mixed = product(matrix(0), split(rows), ((1,), (0,)))
            cosine = table[pl.ds(1280 + 136 * side, 136), :]
            sine = table[pl.ds(1552 + 136 * side, 136), :]
            re, im = mixed[:128], mixed[128:]
            z_re = re * cosine[:128] + im * sine[:128]
            z_im = im * cosine[:128] - re * sine[:128]
            row = lax.broadcasted_iota(jnp.int32, (128, 256), 0)
            z_im = jnp.where(row == 0, 0.0, z_im)
            h_re = im[:8] * cosine[128:]
            h_im = -im[:8] * sine[128:]
            cos_sin.append((z_re, z_im, h_re, h_im))
        flat2 = send2.reshape(2048, 128)
        lane = lax.broadcasted_iota(jnp.int32, (128, 128), 1)
        for parity in range(2):
            if parity == 0:
                z_re, z_im, h_re, h_im = (a + b for a, b in zip(*cos_sin))
            else:
                z_re, z_im, h_re, h_im = (a - b for a, b in zip(*cos_sin))
            right = split(jnp.concatenate([z_re, z_im], axis=0))
            nt = ((1,), (1,))
            by_cos = product(matrix(1 + 2 * parity), right, nt)
            by_sin = product(matrix(2 + 2 * parity), right, nt)
            out_re = by_cos[:, :128] + by_sin[:, 128:]
            out_im = by_cos[:, 128:] - by_sin[:, :128]
            straight = slice(0, 128) if parity == 0 else slice(128, 256)
            mirror = slice(128, 256) if parity == 0 else slice(0, 128)
            middle_c = split(jnp.concatenate([h_re[:1], h_im[:1], jnp.zeros((126, 256), F32)], axis=0))
            middle_s = split(jnp.concatenate([h_im[:1], -h_re[:1], jnp.zeros((126, 256), F32)], axis=0))
            middle = product(matrix(1 + 2 * parity, 128 * parity, 128), middle_c, nt)
            middle = middle + product(matrix(2 + 2 * parity, 128 * parity, 128), middle_s, nt)
            base = 1024 * h + 512 * parity
            flat2[pl.ds(base + 0, 128, stride=4), :] = out_re[straight]
            flat2[pl.ds(base + 2, 128, stride=4), :] = out_im[straight]
            mids[parity] = middle
            mirrors[1 - parity] = (out_re[mirror], -out_im[mirror])
        for parity in range(2):
            base = 1024 * h + 512 * parity
            m_re, m_im = mirrors[parity]
            middle = mids[parity]
            flat2[pl.ds(base + 1, 128, stride=4), :] = jnp.where(lane == 0, middle, m_re)
            flat2[pl.ds(base + 3, 128, stride=4), :] = jnp.where(lane == 0, pltpu.roll(middle, 127, 1), m_im)

    mids, mirrors = {}, {}

    wait(mid1, 0, 1, False)
    over_z(mid1, recv1, 0, 1, False)
    wait(mid1, 0, 0, True)
    over_xy(mid1, recv1, 0, 0, False)
    wait(recv1, 0, 0, False)
    transform(0)
    over_z(send2, mid2, 1, 0, True)
    wait(recv1, 0, 1, True)
    transform(1)
    over_xy(send2, mid2, 1, 1, True)
    wait(mid2, 1, 1, False)
    over_z(mid2, out, 1, 1, False)
    wait(mid2, 1, 0, True)
    over_xy(mid2, out, 1, 0, False)
    def spread(h):
        rows = out.reshape(2048, 128)
        here = pl.ds(256 * h, 256)
        for q in range(4):
            high, low = split(rows[pl.ds(1024 * h + q, 256, stride=4), :])
            place = pl.ds(128 * q, 128)
            plain[0, here, place] = high
            plain[1, here, place] = low

    wait(out, 1, 0, False)
    spread(0)
    power[...] = power_block(plain, 0, 0)
    cross[...] = cross_block(plain, 0, 0)
    wait(out, 1, 1, True)
    spread(1)
    drain()


def exchange(currents):
    table = tables()
    buffer = pltpu.VMEM((2, 16, 16, 4, 128), F32)
    anywhere = pl.BlockSpec(memory_space=pl.ANY)
    dma = pltpu.SemaphoreType.DMA
    return pl.pallas_call(
        exchange_kernel,
        out_shape=(jax.ShapeDtypeStruct((256, 256), F32),) * 2 + (jax.ShapeDtypeStruct((2, 512, 512), BF16),),
        in_specs=[anywhere] * 2,
        out_specs=(pl.BlockSpec(memory_space=pltpu.VMEM),) * 3,
        scratch_shapes=[
            pltpu.VMEM((512, 512), F32),
            pltpu.VMEM(table.shape, F32),
            pltpu.VMEM((1280, 256), BF16),
            pltpu.VMEM((1280, 256), BF16),
            buffer, buffer, buffer, buffer, buffer, buffer,
            dma((3,)), dma((4,)), dma((4,)), dma((4,)), dma((4,)), dma((8,)),
        ],
        compiler_params=pltpu.CompilerParams(collective_id=0, has_side_effects=True, vmem_limit_bytes=54001664),
        name="exchange",
    )(currents, table)


def finish_kernel(power00, cross00, plain, power, cross, blocks, sem):
    copies = []

    def put(source, target, i, j):
        place = target.at[0, pl.ds(256 * i, 256), pl.ds(256 * j, 256)]
        copies.append(pltpu.make_async_copy(source, place, sem.at[len(copies)]))
        copies[-1].start()

    put(power00, power, 0, 0)
    put(cross00, cross, 0, 0)
    blocks[0] = power_block(plain, 0, 1)
    put(blocks.at[0], power, 0, 1)
    blocks[1] = blocks[0].T
    put(blocks.at[1], power, 1, 0)
    blocks[2] = cross_block(plain, 0, 1)
    put(blocks.at[2], cross, 0, 1)
    blocks[3] = -blocks[2].T
    put(blocks.at[3], cross, 1, 0)
    blocks[4] = power_block(plain, 1, 1)
    put(blocks.at[4], power, 1, 1)
    blocks[5] = cross_block(plain, 1, 1)
    put(blocks.at[5], cross, 1, 1)
    for copy in copies:
        copy.wait()


def on_device(currents):
    here = pl.BlockSpec(memory_space=pltpu.VMEM)
    shape = jax.ShapeDtypeStruct((1, 512, 512), F32)
    return pl.pallas_call(
        finish_kernel,
        out_shape=(shape, shape),
        in_specs=[here] * 3,
        out_specs=(pl.BlockSpec(memory_space=pltpu.HBM),) * 2,
        scratch_shapes=[pltpu.VMEM((6, 256, 256), F32), pltpu.SemaphoreType.DMA((8,))],
        compiler_params=pltpu.CompilerParams(vmem_limit_bytes=8 * 1024 * 1024),
        name="finish",
    )(*exchange(currents))


def solution(mesh):
    spec = P(AXES, None, None)
    return jax.shard_map(
        on_device, mesh=mesh, in_specs=(P(AXES, None),), out_specs=(spec, spec), check_vma=False
    )
```

```python
import functools

import jax
import jax.numpy as jnp
import numpy as np
from jax import lax
from jax.experimental import pallas as pl
from jax.experimental.pallas import tpu as pltpu
from jax.sharding import PartitionSpec as P

MESH = pl.DeviceIdType.MESH
AXES = ("gx", "gy", "gz")
STEPS = 131072
F32, BF16 = jnp.float32, jnp.bfloat16
Z_ORDER = [(0, 1), (4, 1), (4, 0), (-3, 1), (3, 1), (-3, 0), (3, 0), (-2, 1), (2, 1), (-2, 0), (2, 0), (-1, 1), (1, 1), (-1, 0), (1, 0)]
XY_ORDER = [
    (1, 0), (-1, 0), (0, 1), (0, -1), (1, 1), (-1, -1), (1, -1), (-1, 1),
    (2, 1), (1, 2), (2, -1), (-1, 2), (2, 0), (0, 2), (2, 2),
]
XY_ORDER = XY_ORDER[::-1]


def tables():
    position = np.arange(256)
    xy, zc = position // 16, position % 16
    x, y = xy // 8 + 2 * (xy // 4 % 2), xy % 4
    z, core = zc // 2, zc % 2
    device = y * 64 + z // 4 * 32 + core * 16 + z % 4 * 4 + x
    r = np.arange(128)
    turn = 2.0 * np.pi / 256
    first = np.concatenate(
        [
            np.cos(turn * (np.outer(r, device) % 256)),
            np.cos(turn * (128 * device % 256))[None],
            -np.sin(turn * (np.outer(r[1:], device) % 256)),
        ]
    )
    m = np.arange(512)
    twist = 2.0 * np.pi / STEPS * np.outer(np.arange(136), m)
    valid = (np.arange(136) <= 128)[:, None]
    twiddle = np.stack([np.cos(twist) * valid, np.sin(twist) * valid])
    twiddle = twiddle.reshape(2, 136, 2, 256).transpose(0, 2, 1, 3).reshape(544, 256)
    even, odd = device[:128], device[128:]
    m = np.arange(256)
    angle_e = 2.0 * np.pi / 512 * (np.outer(np.concatenate([even, 511 - odd]), m) % 512)
    angle_o = 2.0 * np.pi / 512 * (np.outer(np.concatenate([511 - even, odd]), m) % 512)
    second = [f(angle) for angle in (angle_e, angle_o) for f in (np.cos, np.sin)]
    return np.concatenate([first, *second, twiddle]).astype(np.float32)


def split(value):
    high = value.astype(BF16)
    return high, (value - high.astype(F32)).astype(BF16)


def product(a, b, contract):
    def one(left, right):
        return lax.dot_general(left, right, (contract, ((), ())), preferred_element_type=F32)

    return one(a[0], b[0]) + (one(a[0], b[1]) + one(a[1], b[0]))


SCALING = 1.0 / (float(STEPS) * 256.0)
NT = ((1,), (1,))
BOTH, RE, IM = pl.ds(0, 512), pl.ds(0, 256), pl.ds(256, 256)


def modes_of(plain, block, lanes):
    rows = pl.ds(256 * block, 256)
    return plain[0, rows, lanes], plain[1, rows, lanes]


def power_block(plain, i, j):
    return product(modes_of(plain, i, BOTH), modes_of(plain, j, BOTH), NT) * SCALING


def cross_block(plain, i, j):
    cross = product(modes_of(plain, i, IM), modes_of(plain, j, RE), NT)
    other = cross.T if i == j else product(modes_of(plain, i, RE), modes_of(plain, j, IM), NT)
    return (cross - other) * SCALING


def exchange_kernel(
    x_hbm, table_hbm, power, cross, plain,
    x_in, table, high, low, send1, mid1, recv1, send2, mid2, out,
    load_sem, z_send, z_recv, xy_send, xy_recv, own_sem,
):
    load_x = []
    for h in range(2):
        columns = pl.ds(256 * h, 256)
        load_x.append(pltpu.make_async_copy(x_hbm.at[:, columns], x_in.at[:, columns], load_sem.at[h]))
        load_x[h].start()
    y = lax.axis_index("gx")
    gy, gz = lax.axis_index("gy"), lax.axis_index("gz")
    z_hi, core = gy // 2, gy % 2
    z_lo, x = gz // 4, gz % 4
    z = z_hi * 4 + z_lo
    my_zc = z * 2 + core
    my_xy = x % 2 * 8 + x // 2 * 4 + y
    z_peers, xy_peers = [], []
    for dz, dc in Z_ORDER:
        pz = (z + dz + 8) % 8
        pc = 1 - core if dc else core
        z_peers.append((pz * 2 + pc, (y, pz // 4 * 2 + pc, pz % 4 * 4 + x)))
    for dx, dy in XY_ORDER:
        px, py = (x + dx + 4) % 4, (y + dy + 4) % 4
        xy_peers.append((px % 2 * 8 + px // 2 * 4 + py, (py, gy, z_lo * 4 + px)))

    barrier = pltpu.get_barrier_semaphore()
    for _, peer in z_peers + xy_peers:
        pl.semaphore_signal(barrier, inc=1, device_id=peer, device_id_type=MESH)
    load_table = pltpu.make_async_copy(table_hbm, table, load_sem.at[2])
    load_table.start()

    def over_z(source, target, stage, h, target_outer):
        k = stage * 2 + h
        def place(ref):
            return ref.at[h, my_zc] if target_outer else ref.at[h, :, my_zc]
        def send(zc, peer):
            pltpu.make_async_remote_copy(
                src_ref=source.at[h, :, zc], dst_ref=place(target), send_sem=z_send.at[k], recv_sem=z_recv.at[k],
                device_id=peer, device_id_type=MESH,
            ).start()

        if k == 3:
            for pz in (0, 1, 2, 3, 7, 6, 4, 5):
                for pc in (1 - core, core):
                    zc = pz * 2 + pc
                    pl.when(zc != my_zc)(functools.partial(send, zc, (y, pz // 4 * 2 + pc, pz % 4 * 4 + x)))
        else:
            for zc, peer in z_peers:
                send(zc, peer)
        pltpu.make_async_copy(source.at[h, :, my_zc], place(target), own_sem.at[k]).start()

    def over_xy(source, target, stage, h, source_outer):
        k = stage * 2 + h
        def piece(xy):
            return source.at[h, xy] if source_outer else source.at[h, :, xy]
        def send(xy, peer):
            pltpu.make_async_remote_copy(
                src_ref=piece(xy), dst_ref=target.at[h, my_xy], send_sem=xy_send.at[k], recv_sem=xy_recv.at[k],
                device_id=peer, device_id_type=MESH,
            ).start()

        if k == 2:
            for px, py in sorted(((i, j) for i in range(4) for j in range(4)), key=sum):
                xy = px % 2 * 8 + px // 2 * 4 + py
                pl.when(xy != my_xy)(functools.partial(send, xy, (py, gy, z_lo * 4 + px)))
        else:
            for xy, peer in xy_peers:
                send(xy, peer)
        pltpu.make_async_copy(piece(my_xy), target.at[h, my_xy], own_sem.at[4 + k]).start()

    def wait(target, stage, h, is_z):
        k = stage * 2 + h
        send, recv = (z_send, z_recv) if is_z else (xy_send, xy_recv)
        some = target.at[h, pl.ds(0, 15)]
        pltpu.make_async_copy(some, some, recv.at[k]).wait()
        pltpu.make_async_copy(some, some, send.at[k]).wait()
        one = target.at[h, 0]
        pltpu.make_async_copy(one, one, own_sem.at[k if is_z else 4 + k]).wait()

    flat1 = send1.reshape(2048, 128)
    def turn(h):
        load_x[h].wait()
        for k in (2 * h, 2 * h + 1):
            for q in range(4):
                turned = x_in[pl.ds(128 * q, 128), pl.ds(128 * k, 128)].T
                flat1[pl.ds(512 * k + q, 128, stride=4), :] = turned

    turn(0)
    pl.semaphore_wait(barrier, 30)
    over_z(send1, mid1, 0, 0, True)
    turn(1)
    over_xy(send1, mid1, 0, 1, True)
    load_table.wait()
    for i in range(5):
        rows = pl.ds(256 * i, 256)
        high[rows, :], low[rows, :] = split(table[rows, :])

    def matrix(i, start=0, size=256):
        rows = pl.ds(256 * i + start, size)
        return high[rows, :], low[rows, :]

    def transform(h):
        received = recv1.reshape(2048, 128)
        cos_sin = []
        for side in range(2):
            rows = jnp.concatenate(
                [received[pl.ds(1024 * h + 2 * side + q, 256, stride=4), :] for q in range(2)], axis=1
            )
            mixed = product(matrix(0), split(rows), ((1,), (0,)))
            cosine = table[pl.ds(1280 + 136 * side, 136), :]
            sine = table[pl.ds(1552 + 136 * side, 136), :]
            re, im = mixed[:128], mixed[128:]
            z_re = re * cosine[:128] + im * sine[:128]
            z_im = im * cosine[:128] - re * sine[:128]
            row = lax.broadcasted_iota(jnp.int32, (128, 256), 0)
            z_im = jnp.where(row == 0, 0.0, z_im)
            h_re = im[:8] * cosine[128:]
            h_im = -im[:8] * sine[128:]
            cos_sin.append((z_re, z_im, h_re, h_im))
        flat2 = send2.reshape(2048, 128)
        lane = lax.broadcasted_iota(jnp.int32, (128, 128), 1)
        for parity in range(2):
            if parity == 0:
                z_re, z_im, h_re, h_im = (a + b for a, b in zip(*cos_sin))
            else:
                z_re, z_im, h_re, h_im = (a - b for a, b in zip(*cos_sin))
            right = split(jnp.concatenate([z_re, z_im], axis=0))
            nt = ((1,), (1,))
            by_cos = product(matrix(1 + 2 * parity), right, nt)
            by_sin = product(matrix(2 + 2 * parity), right, nt)
            out_re = by_cos[:, :128] + by_sin[:, 128:]
            out_im = by_cos[:, 128:] - by_sin[:, :128]
            straight = slice(0, 128) if parity == 0 else slice(128, 256)
            mirror = slice(128, 256) if parity == 0 else slice(0, 128)
            middle_c = split(jnp.concatenate([h_re[:1], h_im[:1], jnp.zeros((126, 256), F32)], axis=0))
            middle_s = split(jnp.concatenate([h_im[:1], -h_re[:1], jnp.zeros((126, 256), F32)], axis=0))
            middle = product(matrix(1 + 2 * parity, 128 * parity, 128), middle_c, nt)
            middle = middle + product(matrix(2 + 2 * parity, 128 * parity, 128), middle_s, nt)
            base = 1024 * h + 512 * parity
            flat2[pl.ds(base + 0, 128, stride=4), :] = out_re[straight]
            flat2[pl.ds(base + 2, 128, stride=4), :] = out_im[straight]
            mids[parity] = middle
            mirrors[1 - parity] = (out_re[mirror], -out_im[mirror])
        for parity in range(2):
            base = 1024 * h + 512 * parity
            m_re, m_im = mirrors[parity]
            middle = mids[parity]
            flat2[pl.ds(base + 1, 128, stride=4), :] = jnp.where(lane == 0, middle, m_re)
            flat2[pl.ds(base + 3, 128, stride=4), :] = jnp.where(lane == 0, pltpu.roll(middle, 127, 1), m_im)

    mids, mirrors = {}, {}

    wait(mid1, 0, 1, False)
    over_z(mid1, recv1, 0, 1, False)
    wait(mid1, 0, 0, True)
    over_xy(mid1, recv1, 0, 0, False)
    wait(recv1, 0, 0, False)
    transform(0)
    over_z(send2, mid2, 1, 0, True)
    wait(recv1, 0, 1, True)
    transform(1)
    over_xy(send2, mid2, 1, 1, True)
    wait(mid2, 1, 1, False)
    over_z(mid2, out, 1, 1, False)
    wait(mid2, 1, 0, True)
    over_xy(mid2, out, 1, 0, False)
    def spread(h):
        rows = out.reshape(2048, 128)
        here = pl.ds(256 * h, 256)
        for q in range(4):
            high, low = split(rows[pl.ds(1024 * h + q, 256, stride=4), :])
            place = pl.ds(128 * q, 128)
            plain[0, here, place] = high
            plain[1, here, place] = low

    wait(out, 1, 0, False)
    spread(0)
    power[...] = power_block(plain, 0, 0)
    cross[...] = cross_block(plain, 0, 0)
    wait(out, 1, 1, True)
    spread(1)


def exchange(currents):
    table = tables()
    buffer = pltpu.VMEM((2, 16, 16, 4, 128), F32)
    anywhere = pl.BlockSpec(memory_space=pl.ANY)
    dma = pltpu.SemaphoreType.DMA
    return pl.pallas_call(
        exchange_kernel,
        out_shape=(jax.ShapeDtypeStruct((256, 256), F32),) * 2 + (jax.ShapeDtypeStruct((2, 512, 512), BF16),),
        in_specs=[anywhere] * 2,
        out_specs=(pl.BlockSpec(memory_space=pltpu.VMEM),) * 3,
        scratch_shapes=[
            pltpu.VMEM((512, 512), F32),
            pltpu.VMEM(table.shape, F32),
            pltpu.VMEM((1280, 256), BF16),
            pltpu.VMEM((1280, 256), BF16),
            buffer, buffer, buffer, buffer, buffer, buffer,
            dma((3,)), dma((4,)), dma((4,)), dma((4,)), dma((4,)), dma((8,)),
        ],
        compiler_params=pltpu.CompilerParams(collective_id=0, has_side_effects=True, vmem_limit_bytes=54001664),
        name="exchange",
    )(currents, table)


def finish_kernel(power00, cross00, plain, power, cross, blocks, sem):
    copies = []

    def put(source, target, i, j):
        place = target.at[0, pl.ds(256 * i, 256), pl.ds(256 * j, 256)]
        copies.append(pltpu.make_async_copy(source, place, sem.at[len(copies)]))
        copies[-1].start()

    put(power00, power, 0, 0)
    put(cross00, cross, 0, 0)
    blocks[0] = power_block(plain, 0, 1)
    put(blocks.at[0], power, 0, 1)
    blocks[1] = blocks[0].T
    put(blocks.at[1], power, 1, 0)
    blocks[2] = cross_block(plain, 0, 1)
    put(blocks.at[2], cross, 0, 1)
    blocks[3] = -blocks[2].T
    put(blocks.at[3], cross, 1, 0)
    blocks[4] = power_block(plain, 1, 1)
    put(blocks.at[4], power, 1, 1)
    blocks[5] = cross_block(plain, 1, 1)
    put(blocks.at[5], cross, 1, 1)
    for copy in copies:
        copy.wait()


def on_device(currents):
    here = pl.BlockSpec(memory_space=pltpu.VMEM)
    shape = jax.ShapeDtypeStruct((1, 512, 512), F32)
    return pl.pallas_call(
        finish_kernel,
        out_shape=(shape, shape),
        in_specs=[here] * 3,
        out_specs=(pl.BlockSpec(memory_space=pltpu.HBM),) * 2,
        scratch_shapes=[pltpu.VMEM((6, 256, 256), F32), pltpu.SemaphoreType.DMA((8,))],
        compiler_params=pltpu.CompilerParams(vmem_limit_bytes=8 * 1024 * 1024),
        name="finish",
    )(*exchange(currents))


def solution(mesh):
    spec = P(AXES, None, None)
    return jax.shard_map(
        on_device, mesh=mesh, in_specs=(P(AXES, None),), out_specs=(spec, spec), check_vma=False
    )
```
